32 devices in a mesh: slab: 8 (over z, y), pencil: 4 (over x, core).
Axes of the slice: x: 2, y: 2, z: 4, core: 2. Of those that a mesh axis runs over, the one named last changes fastest.
Arguments:
- final_adjoint: bfloat16 [32, 128, 1024], P('slab', 'pencil'), may hold values from -6 to 6
- departure: int32 [4, 32, 128], P(None, 'slab', 'pencil'), may hold values from 1 to 29, as said below
- fraction: float32 [4, 32, 128, 1024], P(None, 'slab', 'pencil'), may hold values from 0 to 1
- image: float32 [32, 128, 1024], P('slab', 'pencil'), may hold values from -6 to 6
Outputs:
- adjoint_start: bfloat16 [32, 128, 1024], P('slab', 'pencil')
- body_force: float32 [3, 32, 128, 1024], P(None, 'slab', 'pencil')
The draws below stay inside these ranges and needn't reach their ends.
Inputs may be any that keep to these rules, and one draw needn't show every extreme that they name: Each base row departure[s][i, j] equals i + d, kept within the volume's range, with an integer displacement d of magnitude at most 4; in every step some blocks have d = 4 and some d = -4.
All inputs are finite; a program needn't handle non-finite values.
Results may differ from the reference program's by a relative error of at most 0.0055.
Values sent between devices are 32-bit elements; how exact they have to be, the bound alone decides.
A program may use at most 64 MiB of HBM per device.

```python
import jax
import jax.numpy as jnp

CX = 4
LINE = 1024
STEPS = 4
NX = 32
NY = 128


def draw_departure(key, part):
    rows = jnp.arange(NX, dtype=jnp.int32)[:, None]

    def one_step(step):
        step_key = jax.random.fold_in(key, step + 101)
        key_stripe, key_jitter, key_pick = jax.random.split(step_key, 3)
        stripe = jax.random.randint(key_stripe, (NY,), -2 * CX, 2 * CX + 1)
        picked = jax.random.permutation(key_pick, NY)
        stripe = stripe.at[picked[0]].set(2 * CX + 1)
        stripe = stripe.at[picked[1]].set(-2 * CX - 1)
        jitter = jax.random.randint(key_jitter, (NX, NY), -1, 2)
        moved = jnp.clip(stripe[None, :] + jitter, -CX, CX)
        return jnp.clip(rows + moved, 1, NX - 3).astype(jnp.int32)
    return jnp.stack([one_step(step) for step in range(STEPS)], axis=0)


def steps_of(rng, dims, shards, least, top_value):
    gain, own = 1.0, jax.random.fold_in(rng, 6)
    for position, parts in shards:
        steps = jnp.exp(jax.random.uniform(jax.random.fold_in(own, position), (parts,), jnp.float32, least / len(shards), top_value / len(shards)))
        gain = gain * jnp.repeat(steps, dims[position] // parts).reshape([-1 if axis == position else 1 for axis in range(len(dims))])
    return gain


def centred(own_key, shape, scale, reach, cuts=(), kind=jnp.bfloat16):
    values = scale * jax.random.normal(own_key, shape, jnp.float32)
    if cuts:
        values = values * steps_of(own_key, shape, cuts, -0.22, 0.18)
    return jnp.clip(values, -reach, reach).astype(kind)


def setup_inputs(seed: int = 0) -> dict:
    key_of = jax.random.split(jax.random.key(seed), 5)
    return {
        "final_adjoint": centred(key_of[0], (NX, NY, LINE), 1.0, 6.0, ((0, 8), (1, 4))),
        "departure": draw_departure(jax.random.fold_in(key_of[4], 71), 0),
        "fraction": jnp.clip(1.0 * jax.random.uniform(key_of[2], (STEPS, NX, NY, LINE), jnp.float32) ** steps_of(key_of[2], (STEPS, NX, NY, LINE), ((1, 8), (2, 4)), -0.2, 0.2), 0.0, 1.0),
        "image": centred(key_of[3], (NX, NY, LINE), 1.0, 6.0, ((0, 8), (1, 4)), jnp.float32),
    }


def spline_weights(fraction):
    rest = 1.0 - fraction
    square = fraction * fraction
    cube = square * fraction
    return (rest * rest * rest / 6.0,
            (3.0 * cube - 6.0 * square + 4.0) / 6.0,
            (-3.0 * cube + 3.0 * square + 3.0 * fraction + 1.0) / 6.0,
            cube / 6.0)


def reference(final_adjoint, departure, fraction, image):
    adjoint = final_adjoint
    column_index = jnp.broadcast_to(jnp.arange(NY, dtype=jnp.int32)[None, :], (NX, NY))
    for step in reversed(range(STEPS)):
        values = adjoint.astype(jnp.float32)
        weights = spline_weights(fraction[step])
        splat = jnp.zeros((NX, NY, LINE), jnp.float32)
        for offset in range(4):
            landing = (departure[step] + (offset - 1)).astype(jnp.int32)
            splat = splat.at[landing, column_index].add(weights[offset] * values)
        adjoint = splat.astype(jnp.bfloat16)
    padded = jnp.pad(image, 1)
    along_first = (padded[2:, 1:-1, 1:-1] - padded[:-2, 1:-1, 1:-1]) * 0.5
    along_second = (padded[1:-1, 2:, 1:-1] - padded[1:-1, :-2, 1:-1]) * 0.5
    along_third = (padded[1:-1, 1:-1, 2:] - padded[1:-1, 1:-1, :-2]) * 0.5
    weight_field = adjoint.astype(jnp.float32)
    body_force = jnp.stack([weight_field * along_first, weight_field * along_second, weight_field * along_third], axis=0)
    return adjoint, body_force
```

```python
import functools

import jax
import jax.numpy as jnp
from jax import lax
from jax.experimental import pallas as pl
from jax.experimental.pallas import tpu as pltpu
from jax.sharding import PartitionSpec as P

BELOW = 5
ABOVE = 6
TILE = 8
MESH = pl.DeviceIdType.MESH


def kernel(
    slabs,
    pencils,
    land_ref,
    adj_ref,
    frac_ref,
    img_ref,
    adj_out,
    grad_out,
    land_buf,
    stage,
    cur,
    frac_buf,
    acc,
    tx_up,
    tx_dn,
    rx_lo,
    rx_hi,
    back_tx,
    back_rx,
    img_pad,
    land_sem,
    cur_sem,
    fl_sem,
    fr_sem,
    up_sem,
    dn_sem,
    back_sem,
    img_sem,
    halo_sem,
):
    s = lax.axis_index("slab")
    p = lax.axis_index("pencil")
    y = lax.rem(s, 2)
    other = 1 - y
    partner = s + 1 - 2 * y
    pair = lax.div(s, 2)
    has_lower = s >= 2
    has_upper = s + 2 < slabs

    rows, cols, line = adj_out.shape
    half = line // 2
    chunks = cols // TILE
    steps = frac_ref.shape[0]
    total = steps * chunks
    tall = 2 * rows
    span = BELOW + tall + ABOVE

    def remote(src, dst, sems, index, where):
        return pltpu.make_async_remote_copy(
            src_ref=src,
            dst_ref=dst,
            send_sem=sems.at[(0,) + index],
            recv_sem=sems.at[(1,) + index],
            device_id=where,
            device_id_type=MESH,
        )

    def frac_block(t, lanes):
        step = steps - 1 - lax.div(t, chunks)
        first = pl.multiple_of(lax.rem(t, chunks) * TILE, TILE)
        return frac_ref.at[step, :, pl.ds(first, TILE), pl.ds(pl.multiple_of(lanes * half, half), half)]

    def frac_local(t):
        return pltpu.make_async_copy(frac_block(t, y), frac_buf.at[t, y], fl_sem.at[t])

    def frac_remote(t, slot):
        return remote(frac_block(t, other), frac_buf.at[t, slot], fr_sem, (t,), {"slab": partner})

    def cur_remote(c, slot):
        return remote(stage.at[other, c], cur.at[c, slot], cur_sem, (c,), {"slab": partner})

    def land_remote(slot):
        return remote(land_ref, land_buf.at[slot], land_sem, (), {"slab": partner})

    def up_copy(t):
        return remote(tx_up.at[t], rx_lo.at[t], up_sem, (t,), {"slab": s + 2})

    def dn_copy(t):
        return remote(tx_dn.at[t], rx_hi.at[t], dn_sem, (t,), {"slab": s - 2})

    def back_copy(c):
        return remote(back_tx.at[c], back_rx.at[c], back_sem, (c,), {"slab": partner})

    center_cols = pl.ds(TILE, cols)
    image_copy = pltpu.make_async_copy(
        img_ref, img_pad.at[pl.ds(1, rows), center_cols], img_sem
    )
    halos = (
        (s + 1 < slabs, s >= 1, remote(
            img_ref.at[pl.ds(rows - 1, 1)], img_pad.at[pl.ds(0, 1), center_cols],
            halo_sem, (0,), {"slab": s + 1})),
        (s >= 1, s + 1 < slabs, remote(
            img_ref.at[pl.ds(0, 1)], img_pad.at[pl.ds(rows + 1, 1), center_cols],
            halo_sem, (1,), {"slab": s - 1})),
        (p + 1 < pencils, p >= 1, remote(
            img_ref.at[:, pl.ds(cols - TILE, TILE)], img_pad.at[pl.ds(1, rows), pl.ds(0, TILE)],
            halo_sem, (2,), {"pencil": p + 1})),
        (p >= 1, p + 1 < pencils, remote(
            img_ref.at[:, pl.ds(0, TILE)], img_pad.at[pl.ds(1, rows), pl.ds(cols + TILE, TILE)],
            halo_sem, (3,), {"pencil": p - 1})),
    )

    barrier = pltpu.get_barrier_semaphore()
    for there, where in (
        (s >= 1, {"slab": s - 1}),
        (s + 1 < slabs, {"slab": s + 1}),
        (has_lower, {"slab": s - 2}),
        (has_upper, {"slab": s + 2}),
        (p >= 1, {"pencil": p - 1}),
        (p + 1 < pencils, {"pencil": p + 1}),
    ):
        @pl.when(there)
        def _():
            pl.semaphore_signal(barrier, inc=1, device_id=where, device_id_type=MESH)

    lax.fori_loop(0, total, lambda t, z: (frac_local(t).start(), z)[1], 0)
    image_copy.start()
    land_buf[y] = land_ref[...]
    for q in range(cols // (2 * TILE)):
        for h in range(2):
            wide = adj_ref[:, 2 * TILE * q : 2 * TILE * (q + 1), half * h : half * (h + 1)]
            wide = wide.astype(jnp.float32)
            stage[h, 2 * q] = wide[:, :TILE]
            stage[h, 2 * q + 1] = wide[:, TILE:]

    peers = sum(
        jnp.where(there, 1, 0)
        for there in (s >= 1, s + 1 < slabs, has_lower, has_upper, p >= 1, p + 1 < pencils)
    )
    pl.semaphore_wait(barrier, peers)

    land_remote(y).start()

    def start_first(c, z):
        cur_remote(c, y).start()
        frac_remote(c, y).start()
        return z

    lax.fori_loop(0, chunks, start_first, 0)
    lax.fori_loop(chunks, total, lambda t, z: (frac_remote(t, y).start(), z)[1], 0)
    for send, _, copy in halos:
        @pl.when(send)
        def _():
            copy.start()

    for c in range(chunks):
        cur[c, y] = stage[y, c]
    land_remote(other).wait_recv()

    def splat(t, c, values):
        frac_local(t).wait()
        frac_remote(t, other).wait_recv()
        parts = []
        hots = []
        target = lax.broadcasted_iota(jnp.int32, (span * TILE, 4 * rows * TILE), 0)
        target = target + (pair * tall - BELOW) * TILE
        for h in range(2):
            f = frac_buf[t, h].reshape(rows * TILE, half)
            v = values[h].reshape(rows * TILE, half)
            rest = 1.0 - f
            square = f * f
            cube = square * f
            sixth = v * (1.0 / 6.0)
            parts.append(rest * rest * rest * sixth)
            parts.append((3.0 * cube - 6.0 * square + 4.0) * sixth)
            parts.append((-3.0 * cube + 3.0 * square + 3.0 * f + 1.0) * sixth)
            parts.append(cube * sixth)
            land = land_buf[h, pl.ds(t, 1), :]
            hots.append(jnp.where(target == land, 1.0, 0.0).astype(jnp.bfloat16))
        hot = jnp.concatenate(hots, axis=1)
        high = [part.astype(jnp.bfloat16) for part in parts]
        low = [(a - b.astype(jnp.float32)).astype(jnp.bfloat16) for a, b in zip(parts, high)]
        out = jnp.dot(hot, jnp.concatenate(high, axis=0), preferred_element_type=jnp.float32)
        out = out + jnp.dot(hot, jnp.concatenate(low, axis=0), preferred_element_type=jnp.float32)
        out = out.reshape(span, TILE, half)
        tx_dn[t] = out[:BELOW]
        tx_up[t] = out[BELOW + tall :]

        @pl.when(has_upper)
        def _():
            up_copy(t).start()

        @pl.when(has_lower)
        def _():
            dn_copy(t).start()

        acc[c] = out[BELOW : BELOW + tall]

    def combine(t, c):
        @pl.when(has_lower)
        def _():
            up_copy(t).wait_recv()
            acc[c, :ABOVE] += rx_lo[t]

        @pl.when(has_upper)
        def _():
            dn_copy(t).wait_recv()
            acc[c, tall - BELOW :] += rx_hi[t]

        whole = acc[c].astype(jnp.bfloat16).astype(jnp.float32)
        return whole.reshape(2, rows, TILE, half)

    def first_step(c, z):
        cur_remote(c, other).wait_recv()
        splat(c, c, cur[c])
        return z

    lax.fori_loop(0, chunks, first_step, 0)

    def later_step(t, z):
        c = lax.rem(t, chunks)
        splat(t, c, combine(t - chunks, c))
        return z

    lax.fori_loop(chunks, total, later_step, 0)

    image_copy.wait()
    for index, (_, receive, copy) in enumerate(halos):
        @pl.when(receive)
        def _():
            copy.wait_recv()

        @pl.when(jnp.logical_not(receive))
        def _():
            if index < 2:
                edge = 0 if index == 0 else rows + 1
                img_pad[edge, TILE : TILE + cols] = jnp.zeros((cols, line), jnp.float32)
            else:
                edge = 0 if index == 2 else cols + TILE
                img_pad[1 : rows + 1, edge : edge + TILE] = jnp.zeros((rows, TILE, line), jnp.float32)

    lane = lax.broadcasted_iota(jnp.int32, (cols, line), 1)

    def gradient(r, z):
        grad_out[0, r] = (img_pad[r + 2, TILE : TILE + cols] - img_pad[r, TILE : TILE + cols]) * 0.5
        grad_out[1, r] = (
            img_pad[r + 1, TILE + 1 : TILE + cols + 1] - img_pad[r + 1, TILE - 1 : TILE + cols - 1]
        ) * 0.5
        center = img_pad[r + 1, TILE : TILE + cols]
        after = jnp.where(lane == line - 1, 0.0, pltpu.roll(center, line - 1, 1))
        before = jnp.where(lane == 0, 0.0, pltpu.roll(center, 1, 1))
        grad_out[2, r] = (after - before) * 0.5
        return z

    lax.fori_loop(0, rows, gradient, 0)

    def finish(c, z):
        combine_out = combine(total - chunks + c, c)
        acc[c] = combine_out.reshape(tall, TILE, half)
        back_tx[c] = acc[c, pl.ds(other * rows, rows)]
        back_copy(c).start()
        first = pl.multiple_of(c * TILE, TILE)
        adj_out[:, pl.ds(first, TILE), pl.ds(pl.multiple_of(y * half, half), half)] = acc[c, pl.ds(y * rows, rows)]
        return z

    lax.fori_loop(0, chunks, finish, 0)

    def collect(c, z):
        back_copy(c).wait_recv()
        first = pl.multiple_of(c * TILE, TILE)
        adj_out[:, pl.ds(first, TILE), pl.ds(pl.multiple_of(other * half, half), half)] = back_rx[c]
        return z

    lax.fori_loop(0, chunks, collect, 0)

    land_remote(y).wait_send()
    lax.fori_loop(0, chunks, lambda c, z: (cur_remote(c, y).wait_send(), back_copy(c).wait_send(), z)[2], 0)

    def drain(t, z):
        frac_remote(t, y).wait_send()

        @pl.when(has_upper)
        def _():
            up_copy(t).wait_send()

        @pl.when(has_lower)
        def _():
            dn_copy(t).wait_send()

        return z

    lax.fori_loop(0, total, drain, 0)
    for send, _, copy in halos:
        @pl.when(send)
        def _():
            copy.wait_send()


def shards(slabs, pencils, final_adjoint, departure, fraction, image):
    steps, rows, cols = departure.shape
    line = image.shape[2]
    half = line // 2
    chunks = cols // TILE
    total = steps * chunks
    tall = 2 * rows
    assert slabs % 2 == 0 and ABOVE <= tall and cols % (2 * TILE) == 0 and half % 128 == 0

    land = departure[::-1].reshape(steps, rows, chunks, TILE).transpose(0, 2, 1, 3)
    land = land[:, :, None] + (jnp.arange(4, dtype=jnp.int32) - 1)[:, None, None]
    land = (land * TILE + jnp.arange(TILE, dtype=jnp.int32)).reshape(total, 4 * rows * TILE)

    f32 = jnp.float32
    dma = pltpu.SemaphoreType.DMA
    vmem = pl.BlockSpec(memory_space=pltpu.VMEM)
    hbm = pl.BlockSpec(memory_space=pl.ANY)
    adjoint, gradient = pl.pallas_call(
        functools.partial(kernel, slabs, pencils),
        name="splat",
        out_shape=(
            jax.ShapeDtypeStruct((rows, cols, line), f32),
            jax.ShapeDtypeStruct((3, rows, cols, line), f32),
        ),
        in_specs=[vmem, vmem, hbm, hbm],
        out_specs=(vmem, vmem),
        scratch_shapes=[
            pltpu.VMEM((2, total, 4 * rows * TILE), jnp.int32),
            pltpu.VMEM((2, chunks, rows, TILE, half), f32),
            pltpu.VMEM((chunks, 2, rows, TILE, half), f32),
            pltpu.VMEM((total, 2, rows, TILE, half), f32),
            pltpu.VMEM((chunks, tall, TILE, half), f32),
            pltpu.VMEM((total, ABOVE, TILE, half), f32),
            pltpu.VMEM((total, BELOW, TILE, half), f32),
            pltpu.VMEM((total, ABOVE, TILE, half), f32),
            pltpu.VMEM((total, BELOW, TILE, half), f32),
            pltpu.VMEM((chunks, rows, TILE, half), f32),
            pltpu.VMEM((chunks, rows, TILE, half), f32),
            pltpu.VMEM((rows + 2, cols + 2 * TILE, line), f32),
            dma((2,)),
            dma((2, chunks)),
            dma((total,)),
            dma((2, total)),
            dma((2, total)),
            dma((2, total)),
            dma((2, chunks)),
            dma(()),
            dma((2, 4)),
        ],
        compiler_params=pltpu.CompilerParams(
            collective_id=0, has_side_effects=True, vmem_limit_bytes=40 * 1024 * 1024
        ),
    )(land, final_adjoint, fraction, image)
    return adjoint.astype(jnp.bfloat16), adjoint[None] * gradient


def solution(mesh):
    in_specs = (
        P("slab", "pencil", None),
        P(None, "slab", "pencil"),
        P(None, "slab", "pencil", None),
        P("slab", "pencil", None),
    )
    out_specs = (P("slab", "pencil", None), P(None, "slab", "pencil", None))
    body = functools.partial(shards, mesh.shape["slab"], mesh.shape["pencil"])
    return jax.shard_map(body, mesh=mesh, in_specs=in_specs, out_specs=out_specs, check_vma=False)
```

```python
import functools

import jax
import jax.numpy as jnp
from jax import lax
from jax.experimental import pallas as pl
from jax.experimental.pallas import tpu as pltpu
from jax.sharding import PartitionSpec as P

BELOW = 5
ABOVE = 6
TILE = 8
WIDTH = 256
MESH = pl.DeviceIdType.MESH


def kernel(
    slabs,
    pencils,
    dep_ref,
    adj_ref,
    frac_ref,
    img_ref,
    adj_out,
    grad_out,
    dep_buf,
    land_buf,
    adj_buf,
    stage,
    cur,
    frac_buf,
    acc,
    tx_up,
    tx_dn,
    rx_lo,
    rx_hi,
    back_tx,
    back_rx,
    img_pad,
    dep_sem,
    adj_sem,
    cur_sem,
    fl_sem,
    fr_sem,
    up_sem,
    dn_sem,
    back_sem,
    img_sem,
    halo_sem,
):
    s = lax.axis_index("slab")
    p = lax.axis_index("pencil")
    y = lax.rem(s, 2)
    other = 1 - y
    partner = s + 1 - 2 * y
    pair = lax.div(s, 2)
    has_lower = s >= 2
    has_upper = s + 2 < slabs

    rows, cols, line = adj_out.shape
    half = line // 2
    width = stage.shape[-1]
    lanes_parts = half // width
    tiles = cols // TILE
    chunks = tiles * lanes_parts
    steps = frac_ref.shape[0]
    total = steps * chunks
    tall = 2 * rows
    span = BELOW + tall + ABOVE

    def remote(src, dst, sems, index, where):
        return pltpu.make_async_remote_copy(
            src_ref=src,
            dst_ref=dst,
            send_sem=sems.at[(0,) + index],
            recv_sem=sems.at[(1,) + index],
            device_id=where,
            device_id_type=MESH,
        )

    def place(c, side):
        first = pl.multiple_of(lax.div(c, lanes_parts) * TILE, TILE)
        lanes = pl.multiple_of(side * half + lax.rem(c, lanes_parts) * width, width)
        return pl.ds(first, TILE), pl.ds(lanes, width)

    def frac_block(t, side):
        step = steps - 1 - lax.div(t, chunks)
        return frac_ref.at[(step, slice(None)) + place(lax.rem(t, chunks), side)]

    def frac_local(t):
        return pltpu.make_async_copy(frac_block(t, y), frac_buf.at[t, y], fl_sem.at[t])

    def frac_remote(t, slot):
        return remote(frac_block(t, other), frac_buf.at[t, slot], fr_sem, (t,), {"slab": partner})

    def cur_remote(c, slot):
        return remote(stage.at[other, c], cur.at[c, slot], cur_sem, (c,), {"slab": partner})

    def dep_remote(slot):
        return remote(dep_ref, dep_buf.at[slot], dep_sem, (), {"slab": partner})

    def up_copy(t):
        return remote(tx_up.at[t], rx_lo.at[t], up_sem, (t,), {"slab": s + 2})

    def dn_copy(t):
        return remote(tx_dn.at[t], rx_hi.at[t], dn_sem, (t,), {"slab": s - 2})

    def back_copy(c):
        return remote(back_tx.at[c], back_rx.at[c], back_sem, (c,), {"slab": partner})

    center_cols = pl.ds(TILE, cols)
    image_copy = pltpu.make_async_copy(
        img_ref, img_pad.at[pl.ds(1, rows), center_cols], img_sem
    )
    halos = (
        (s + 1 < slabs, s >= 1, remote(
            img_ref.at[pl.ds(rows - 1, 1)], img_pad.at[pl.ds(0, 1), center_cols],
            halo_sem, (0,), {"slab": s + 1})),
        (s >= 1, s + 1 < slabs, remote(
            img_ref.at[pl.ds(0, 1)], img_pad.at[pl.ds(rows + 1, 1), center_cols],
            halo_sem, (1,), {"slab": s - 1})),
        (p + 1 < pencils, p >= 1, remote(
            img_ref.at[:, pl.ds(cols - TILE, TILE)], img_pad.at[pl.ds(1, rows), pl.ds(0, TILE)],
            halo_sem, (2,), {"pencil": p + 1})),
        (p >= 1, p + 1 < pencils, remote(
            img_ref.at[:, pl.ds(0, TILE)], img_pad.at[pl.ds(1, rows), pl.ds(cols + TILE, TILE)],
            halo_sem, (3,), {"pencil": p - 1})),
    )

    barrier = pltpu.get_barrier_semaphore()
    for there, where in (
        (s >= 1, {"slab": s - 1}),
        (s + 1 < slabs, {"slab": s + 1}),
        (has_lower, {"slab": s - 2}),
        (has_upper, {"slab": s + 2}),
        (p >= 1, {"pencil": p - 1}),
        (p + 1 < pencils, {"pencil": p + 1}),
    ):
        @pl.when(there)
        def _():
            pl.semaphore_signal(barrier, inc=1, device_id=where, device_id_type=MESH)

    adj_copy = pltpu.make_async_copy(adj_ref, adj_buf, adj_sem)
    adj_copy.start()
    lax.fori_loop(0, total, lambda t, z: (frac_local(t).start(), z)[1], 0)
    image_copy.start()
    dep_buf[y] = dep_ref[...]
    adj_copy.wait()
    for q in range(cols // (2 * TILE)):
        for h in range(2):
            for k in range(lanes_parts):
                first = half * h + width * k
                wide = adj_buf[:, 2 * TILE * q : 2 * TILE * (q + 1), first : first + width]
                wide = wide.astype(jnp.float32)
                stage[h, 2 * q * lanes_parts + k] = wide[:, :TILE]
                stage[h, (2 * q + 1) * lanes_parts + k] = wide[:, TILE:]

    peers = sum(
        jnp.where(there, 1, 0)
        for there in (s >= 1, s + 1 < slabs, has_lower, has_upper, p >= 1, p + 1 < pencils)
    )
    pl.semaphore_wait(barrier, peers)

    dep_remote(y).start()

    def start_first(c, z):
        frac_remote(c, y).start()
        cur_remote(c, y).start()
        return z

    lax.fori_loop(0, chunks, start_first, 0)
    lax.fori_loop(chunks, total, lambda t, z: (frac_remote(t, y).start(), z)[1], 0)
    for send, _, copy in halos:
        @pl.when(send)
        def _():
            copy.start()

    for c in range(chunks):
        cur[c, y] = stage[y, c]

    lane = lax.broadcasted_iota(jnp.int32, (steps, 4 * rows * TILE), 1)
    lane_row = lax.rem(lax.div(lane, TILE), rows)
    fixed = lane_row + lax.div(lane, rows * TILE) - 1 + BELOW
    fixed = fixed * TILE + lax.rem(lane, TILE)
    pick_lane = lax.broadcasted_iota(jnp.int32, (cols, 4 * rows * TILE), 1)
    pick_col = lax.broadcasted_iota(jnp.int32, (cols, 4 * rows * TILE), 0)
    keep_lane = lax.broadcasted_iota(jnp.int32, (steps * rows, 4 * rows * TILE), 1)
    keep_row = lax.broadcasted_iota(jnp.int32, (steps * rows, 4 * rows * TILE), 0)
    keep = lax.rem(keep_row, rows) == lax.rem(lax.div(keep_lane, TILE), rows)
    group_step = lax.broadcasted_iota(jnp.int32, (steps, steps * rows), 0)
    group_row = lax.broadcasted_iota(jnp.int32, (steps, steps * rows), 1)
    group = jnp.where(group_step == lax.div(group_row, rows), 1.0, 0.0).astype(jnp.bfloat16)
    row_of = lax.broadcasted_iota(jnp.int32, (rows, cols), 0)

    def landing(h):
        first_row = pair * tall + h * rows
        moved = jnp.concatenate([dep_buf[h, k] - row_of - first_row for k in range(steps)], axis=0)
        moved = moved.astype(jnp.float32).astype(jnp.bfloat16)
        for tile in range(tiles):
            pick = pick_col == tile * TILE + lax.rem(pick_lane, TILE)
            pick = jnp.where(pick, 1.0, 0.0).astype(jnp.bfloat16)
            spread = jnp.dot(moved, pick, preferred_element_type=jnp.float32)
            spread = jnp.where(keep, spread, 0.0).astype(jnp.bfloat16)
            by_step = jnp.dot(group, spread, preferred_element_type=jnp.float32)
            land_buf[h, tile] = fixed + h * rows * TILE + by_step.astype(jnp.int32) * TILE

    landing(y)
    dep_remote(other).wait_recv()
    landing(other)

    def splat(t, c, values):
        frac_local(t).wait()
        frac_remote(t, other).wait_recv()
        parts = []
        hots = []
        target = lax.broadcasted_iota(jnp.int32, (span * TILE, 4 * rows * TILE), 0)
        tile = lax.div(c, lanes_parts)
        step = steps - 1 - lax.div(t, chunks)
        for h in range(2):
            f = frac_buf[t, h].reshape(rows * TILE, width)
            v = values[h].reshape(rows * TILE, width)
            rest = 1.0 - f
            square = f * f
            cube = square * f
            sixth = v * (1.0 / 6.0)
            parts.append(rest * rest * rest * sixth)
            parts.append((3.0 * cube - 6.0 * square + 4.0) * sixth)
            parts.append((-3.0 * cube + 3.0 * square + 3.0 * f + 1.0) * sixth)
            parts.append(cube * sixth)
            land = land_buf[h, tile, pl.ds(step, 1), :]
            hots.append(jnp.where(target == land, 1.0, 0.0).astype(jnp.bfloat16))
        hot = jnp.concatenate(hots, axis=1)
        high = [part.astype(jnp.bfloat16) for part in parts]
        low = [(a - b.astype(jnp.float32)).astype(jnp.bfloat16) for a, b in zip(parts, high)]
        out = jnp.dot(hot, jnp.concatenate(high, axis=0), preferred_element_type=jnp.float32)
        out = out + jnp.dot(hot, jnp.concatenate(low, axis=0), preferred_element_type=jnp.float32)
        out = out.reshape(span, TILE, width)
        tx_dn[t] = out[:BELOW]
        tx_up[t] = out[BELOW + tall :]

        @pl.when(has_upper)
        def _():
            up_copy(t).start()

        @pl.when(has_lower)
        def _():
            dn_copy(t).start()

        acc[c] = out[BELOW : BELOW + tall]

    def combine(t, c):
        @pl.when(has_lower)
        def _():
            up_copy(t).wait_recv()
            acc[c, :ABOVE] += rx_lo[t]

        @pl.when(has_upper)
        def _():
            dn_copy(t).wait_recv()
            acc[c, tall - BELOW :] += rx_hi[t]

        whole = acc[c].astype(jnp.bfloat16).astype(jnp.float32)
        return whole.reshape(2, rows, TILE, width)

    def first_step(c, z):
        cur_remote(c, other).wait_recv()
        splat(c, c, cur[c])
        return z

    lax.fori_loop(0, chunks, first_step, 0)

    def later_step(t, z):
        c = lax.rem(t, chunks)
        splat(t, c, combine(t - chunks, c))
        return z

    lax.fori_loop(chunks, total, later_step, 0)

    image_copy.wait()
    for index, (_, receive, copy) in enumerate(halos):
        @pl.when(receive)
        def _():
            copy.wait_recv()

        @pl.when(jnp.logical_not(receive))
        def _():
            if index < 2:
                edge = 0 if index == 0 else rows + 1
                img_pad[edge, TILE : TILE + cols] = jnp.zeros((cols, line), jnp.float32)
            else:
                edge = 0 if index == 2 else cols + TILE
                img_pad[1 : rows + 1, edge : edge + TILE] = jnp.zeros((rows, TILE, line), jnp.float32)

    lane = lax.broadcasted_iota(jnp.int32, (cols, line), 1)

    def gradient(r, z):
        grad_out[0, r] = (img_pad[r + 2, TILE : TILE + cols] - img_pad[r, TILE : TILE + cols]) * 0.5
        grad_out[1, r] = (
            img_pad[r + 1, TILE + 1 : TILE + cols + 1] - img_pad[r + 1, TILE - 1 : TILE + cols - 1]
        ) * 0.5
        center = img_pad[r + 1, TILE : TILE + cols]
        after = jnp.where(lane == line - 1, 0.0, pltpu.roll(center, line - 1, 1))
        before = jnp.where(lane == 0, 0.0, pltpu.roll(center, 1, 1))
        grad_out[2, r] = (after - before) * 0.5
        return z

    lax.fori_loop(0, rows, gradient, 0)

    def finish(c, z):
        combine_out = combine(total - chunks + c, c)
        acc[c] = combine_out.reshape(tall, TILE, width)
        back_tx[c] = acc[c, pl.ds(other * rows, rows)]
        back_copy(c).start()
        adj_out[(slice(None),) + place(c, y)] = acc[c, pl.ds(y * rows, rows)]
        return z

    lax.fori_loop(0, chunks, finish, 0)

    def collect(c, z):
        back_copy(c).wait_recv()
        adj_out[(slice(None),) + place(c, other)] = back_rx[c]
        return z

    lax.fori_loop(0, chunks, collect, 0)

    dep_remote(y).wait_send()
    lax.fori_loop(0, chunks, lambda c, z: (cur_remote(c, y).wait_send(), back_copy(c).wait_send(), z)[2], 0)

    def drain(t, z):
        frac_remote(t, y).wait_send()

        @pl.when(has_upper)
        def _():
            up_copy(t).wait_send()

        @pl.when(has_lower)
        def _():
            dn_copy(t).wait_send()

        return z

    lax.fori_loop(0, total, drain, 0)
    for send, _, copy in halos:
        @pl.when(send)
        def _():
            copy.wait_send()


def shards(slabs, pencils, final_adjoint, departure, fraction, image):
    steps, rows, cols = departure.shape
    line = image.shape[2]
    half = line // 2
    width = WIDTH if half % WIDTH == 0 else half
    tiles = cols // TILE
    chunks = tiles * (half // width)
    total = steps * chunks
    tall = 2 * rows
    assert slabs % 2 == 0 and ABOVE <= tall and cols % (2 * TILE) == 0 and half % 128 == 0

    f32 = jnp.float32
    dma = pltpu.SemaphoreType.DMA
    vmem = pl.BlockSpec(memory_space=pltpu.VMEM)
    hbm = pl.BlockSpec(memory_space=pltpu.HBM)
    adjoint, gradient = pl.pallas_call(
        functools.partial(kernel, slabs, pencils),
        name="splat",
        out_shape=(
            jax.ShapeDtypeStruct((rows, cols, line), f32),
            jax.ShapeDtypeStruct((3, rows, cols, line), f32),
        ),
        in_specs=[vmem, hbm, hbm, hbm],
        out_specs=(vmem, vmem),
        scratch_shapes=[
            pltpu.VMEM((2, steps, rows, cols), jnp.int32),
            pltpu.VMEM((2, tiles, steps, 4 * rows * TILE), jnp.int32),
            pltpu.VMEM((rows, cols, line), jnp.bfloat16),
            pltpu.VMEM((2, chunks, rows, TILE, width), f32),
            pltpu.VMEM((chunks, 2, rows, TILE, width), f32),
            pltpu.VMEM((total, 2, rows, TILE, width), f32),
            pltpu.VMEM((chunks, tall, TILE, width), f32),
            pltpu.VMEM((total, ABOVE, TILE, width), f32),
            pltpu.VMEM((total, BELOW, TILE, width), f32),
            pltpu.VMEM((total, ABOVE, TILE, width), f32),
            pltpu.VMEM((total, BELOW, TILE, width), f32),
            pltpu.VMEM((chunks, rows, TILE, width), f32),
            pltpu.VMEM((chunks, rows, TILE, width), f32),
            pltpu.VMEM((rows + 2, cols + 2 * TILE, line), f32),
            dma((2,)),
            dma(()),
            dma((2, chunks)),
            dma((total,)),
            dma((2, total)),
            dma((2, total)),
            dma((2, total)),
            dma((2, chunks)),
            dma(()),
            dma((2, 4)),
        ],
        compiler_params=pltpu.CompilerParams(
            collective_id=0, has_side_effects=True, vmem_limit_bytes=40 * 1024 * 1024
        ),
    )(departure, final_adjoint, fraction, image)
    return adjoint.astype(jnp.bfloat16), adjoint[None] * gradient


def solution(mesh):
    in_specs = (
        P("slab", "pencil", None),
        P(None, "slab", "pencil"),
        P(None, "slab", "pencil", None),
        P("slab", "pencil", None),
    )
    out_specs = (P("slab", "pencil", None), P(None, "slab", "pencil", None))
    body = functools.partial(shards, mesh.shape["slab"], mesh.shape["pencil"])
    return jax.shard_map(body, mesh=mesh, in_specs=in_specs, out_specs=out_specs, check_vma=False)
```

```python
import functools

import jax
import jax.numpy as jnp
from jax import lax
from jax.experimental import pallas as pl
from jax.experimental.pallas import tpu as pltpu
from jax.sharding import PartitionSpec as P

BELOW = 5
ABOVE = 6
TILE = 8
AHEAD = 4
WIDTH = 256
MESH = pl.DeviceIdType.MESH


def kernel(
    slabs,
    pencils,
    dep_ref,
    adj_ref,
    frac_ref,
    img_ref,
    adj_out,
    grad_out,
    dep_buf,
    land_buf,
    adj_buf,
    stage,
    cur,
    frac_buf,
    acc,
    tx_up,
    tx_dn,
    rx_lo,
    rx_hi,
    back_tx,
    back_rx,
    img_pad,
    dep_sem,
    own_dep_sem,
    adj_sem,
    cur_sem,
    fl_sem,
    fr_sem,
    up_sem,
    dn_sem,
    back_sem,
    img_sem,
    halo_sem,
):
    s = lax.axis_index("slab")
    p = lax.axis_index("pencil")
    y = lax.rem(s, 2)
    other = 1 - y
    partner = s + 1 - 2 * y
    pair = lax.div(s, 2)
    has_lower = s >= 2
    has_upper = s + 2 < slabs

    rows, cols, line = adj_out.shape
    half = line // 2
    width = stage.shape[-1]
    lanes_parts = half // width
    tiles = cols // TILE
    chunks = tiles * lanes_parts
    steps = frac_ref.shape[0]
    total = steps * chunks
    ahead = chunks + chunks * AHEAD // 8
    tall = 2 * rows
    span = BELOW + tall + ABOVE

    def remote(src, dst, sems, index, where):
        return pltpu.make_async_remote_copy(
            src_ref=src,
            dst_ref=dst,
            send_sem=sems.at[(0,) + index],
            recv_sem=sems.at[(1,) + index],
            device_id=where,
            device_id_type=MESH,
        )

    def place(c, side):
        first = pl.multiple_of(lax.div(c, lanes_parts) * TILE, TILE)
        lanes = pl.multiple_of(side * half + lax.rem(c, lanes_parts) * width, width)
        return pl.ds(first, TILE), pl.ds(lanes, width)

    def frac_block(t, side):
        step = steps - 1 - lax.div(t, chunks)
        return frac_ref.at[(step, slice(None)) + place(lax.rem(t, chunks), side)]

    def frac_local(t):
        return pltpu.make_async_copy(frac_block(t, y), frac_buf.at[t, y], fl_sem.at[t])

    def frac_remote(t, slot):
        return remote(frac_block(t, other), frac_buf.at[t, slot], fr_sem, (t,), {"slab": partner})

    def cur_remote(c, slot):
        return remote(stage.at[other, c], cur.at[c, slot], cur_sem, (c,), {"slab": partner})

    def dep_remote(slot):
        return remote(dep_ref, dep_buf.at[slot], dep_sem, (), {"slab": partner})

    def up_copy(t):
        return remote(tx_up.at[t], rx_lo.at[t], up_sem, (t,), {"slab": s + 2})

    def dn_copy(t):
        return remote(tx_dn.at[t], rx_hi.at[t], dn_sem, (t,), {"slab": s - 2})

    def back_copy(c):
        return remote(back_tx.at[c], back_rx.at[c], back_sem, (c,), {"slab": partner})

    center_cols = pl.ds(TILE, cols)
    image_copy = pltpu.make_async_copy(
        img_ref, img_pad.at[pl.ds(1, rows), center_cols], img_sem
    )
    halos = (
        (s + 1 < slabs, s >= 1, remote(
            img_ref.at[pl.ds(rows - 1, 1)], img_pad.at[pl.ds(0, 1), center_cols],
            halo_sem, (0,), {"slab": s + 1})),
        (s >= 1, s + 1 < slabs, remote(
            img_ref.at[pl.ds(0, 1)], img_pad.at[pl.ds(rows + 1, 1), center_cols],
            halo_sem, (1,), {"slab": s - 1})),
        (p + 1 < pencils, p >= 1, remote(
            img_ref.at[:, pl.ds(cols - TILE, TILE)], img_pad.at[pl.ds(1, rows), pl.ds(0, TILE)],
            halo_sem, (2,), {"pencil": p + 1})),
        (p >= 1, p + 1 < pencils, remote(
            img_ref.at[:, pl.ds(0, TILE)], img_pad.at[pl.ds(1, rows), pl.ds(cols + TILE, TILE)],
            halo_sem, (3,), {"pencil": p - 1})),
    )

    barrier = pltpu.get_barrier_semaphore()
    for there, where in (
        (s >= 1, {"slab": s - 1}),
        (s + 1 < slabs, {"slab": s + 1}),
        (has_lower, {"slab": s - 2}),
        (has_upper, {"slab": s + 2}),
        (p >= 1, {"pencil": p - 1}),
        (p + 1 < pencils, {"pencil": p + 1}),
    ):
        @pl.when(there)
        def _():
            pl.semaphore_signal(barrier, inc=1, device_id=where, device_id_type=MESH)

    adj_copy = pltpu.make_async_copy(adj_ref, adj_buf, adj_sem)
    dep_copy = pltpu.make_async_copy(dep_ref, dep_buf.at[y], own_dep_sem)
    dep_copy.start()
    adj_copy.start()
    lax.fori_loop(0, total, lambda t, z: (frac_local(t).start(), z)[1], 0)
    image_copy.start()
    adj_copy.wait()
    for q in range(cols // (2 * TILE)):
        for h in range(2):
            for k in range(lanes_parts):
                first = half * h + width * k
                wide = adj_buf[:, 2 * TILE * q : 2 * TILE * (q + 1), first : first + width]
                wide = wide.astype(jnp.float32)
                stage[h, 2 * q * lanes_parts + k] = wide[:, :TILE]
                stage[h, (2 * q + 1) * lanes_parts + k] = wide[:, TILE:]

    peers = sum(
        jnp.where(there, 1, 0)
        for there in (s >= 1, s + 1 < slabs, has_lower, has_upper, p >= 1, p + 1 < pencils)
    )
    pl.semaphore_wait(barrier, peers)

    dep_remote(y).start()

    def start_first(c, z):
        frac_remote(c, y).start()
        cur_remote(c, y).start()
        return z

    lax.fori_loop(0, chunks, start_first, 0)
    lax.fori_loop(chunks, ahead, lambda t, z: (frac_remote(t, y).start(), z)[1], 0)

    for c in range(chunks):
        cur[c, y] = stage[y, c]

    lane = lax.broadcasted_iota(jnp.int32, (steps, 4 * rows * TILE), 1)
    lane_row = lax.rem(lax.div(lane, TILE), rows)
    fixed = lane_row + lax.div(lane, rows * TILE) - 1 + BELOW
    fixed = fixed * TILE + lax.rem(lane, TILE)
    pick_lane = lax.broadcasted_iota(jnp.int32, (cols, 4 * rows * TILE), 1)
    pick_col = lax.broadcasted_iota(jnp.int32, (cols, 4 * rows * TILE), 0)
    keep_lane = lax.broadcasted_iota(jnp.int32, (steps * rows, 4 * rows * TILE), 1)
    keep_row = lax.broadcasted_iota(jnp.int32, (steps * rows, 4 * rows * TILE), 0)
    keep = lax.rem(keep_row, rows) == lax.rem(lax.div(keep_lane, TILE), rows)
    group_step = lax.broadcasted_iota(jnp.int32, (steps, steps * rows), 0)
    group_row = lax.broadcasted_iota(jnp.int32, (steps, steps * rows), 1)
    group = jnp.where(group_step == lax.div(group_row, rows), 1.0, 0.0).astype(jnp.bfloat16)
    row_of = lax.broadcasted_iota(jnp.int32, (rows, cols), 0)

    def landing(h):
        first_row = pair * tall + h * rows
        moved = jnp.concatenate([dep_buf[h, k] - row_of - first_row for k in range(steps)], axis=0)
        moved = moved.astype(jnp.float32).astype(jnp.bfloat16)
        for tile in range(tiles):
            pick = pick_col == tile * TILE + lax.rem(pick_lane, TILE)
            pick = jnp.where(pick, 1.0, 0.0).astype(jnp.bfloat16)
            spread = jnp.dot(moved, pick, preferred_element_type=jnp.float32)
            spread = jnp.where(keep, spread, 0.0).astype(jnp.bfloat16)
            by_step = jnp.dot(group, spread, preferred_element_type=jnp.float32)
            land_buf[h, tile] = fixed + h * rows * TILE + by_step.astype(jnp.int32) * TILE

    dep_copy.wait()
    landing(y)
    dep_remote(other).wait_recv()
    landing(other)

    def splat(t, c, values):
        frac_local(t).wait()
        frac_remote(t, other).wait_recv()
        parts = []
        hots = []
        target = lax.broadcasted_iota(jnp.int32, (span * TILE, 4 * rows * TILE), 0)
        tile = lax.div(c, lanes_parts)
        step = steps - 1 - lax.div(t, chunks)
        for h in range(2):
            f = frac_buf[t, h].reshape(rows * TILE, width)
            v = values[h].reshape(rows * TILE, width)
            rest = 1.0 - f
            square = f * f
            cube = square * f
            sixth = v * (1.0 / 6.0)
            parts.append(rest * rest * rest * sixth)
            parts.append((3.0 * cube - 6.0 * square + 4.0) * sixth)
            parts.append((-3.0 * cube + 3.0 * square + 3.0 * f + 1.0) * sixth)
            parts.append(cube * sixth)
            land = land_buf[h, tile, pl.ds(step, 1), :]
            hots.append(jnp.where(target == land, 1.0, 0.0).astype(jnp.bfloat16))
        hot = jnp.concatenate(hots, axis=1)
        high = [part.astype(jnp.bfloat16) for part in parts]
        low = [(a - b.astype(jnp.float32)).astype(jnp.bfloat16) for a, b in zip(parts, high)]
        out = jnp.dot(hot, jnp.concatenate(high, axis=0), preferred_element_type=jnp.float32)
        out = out + jnp.dot(hot, jnp.concatenate(low, axis=0), preferred_element_type=jnp.float32)
        out = out.reshape(span, TILE, width)
        tx_dn[t] = out[:BELOW]
        tx_up[t] = out[BELOW + tall :]

        @pl.when(has_upper)
        def _():
            up_copy(t).start()

        @pl.when(has_lower)
        def _():
            dn_copy(t).start()

        acc[c] = out[BELOW : BELOW + tall]

    def combine(t, c):
        @pl.when(has_lower)
        def _():
            up_copy(t).wait_recv()
            acc[c, :ABOVE] += rx_lo[t]

        @pl.when(has_upper)
        def _():
            dn_copy(t).wait_recv()
            acc[c, tall - BELOW :] += rx_hi[t]

        whole = acc[c].astype(jnp.bfloat16).astype(jnp.float32)
        return whole.reshape(2, rows, TILE, width)

    def first_step(c, z):
        cur_remote(c, other).wait_recv()
        splat(c, c, cur[c])
        frac_remote(c + ahead, y).start()
        return z

    lax.fori_loop(0, chunks, first_step, 0)

    def later_step(t, z):
        c = lax.rem(t, chunks)
        splat(t, c, combine(t - chunks, c))
        return z

    def paced_step(t, z):
        frac_remote(t + ahead, y).start()
        return later_step(t, z)

    lax.fori_loop(chunks, total - ahead, paced_step, 0)
    for send, _, copy in halos:
        @pl.when(send)
        def _():
            copy.start()

    lax.fori_loop(total - ahead, total, later_step, 0)

    image_copy.wait()
    for index, (_, receive, copy) in enumerate(halos):
        @pl.when(receive)
        def _():
            copy.wait_recv()

        @pl.when(jnp.logical_not(receive))
        def _():
            if index < 2:
                edge = 0 if index == 0 else rows + 1
                img_pad[edge, TILE : TILE + cols] = jnp.zeros((cols, line), jnp.float32)
            else:
                edge = 0 if index == 2 else cols + TILE
                img_pad[1 : rows + 1, edge : edge + TILE] = jnp.zeros((rows, TILE, line), jnp.float32)

    lane = lax.broadcasted_iota(jnp.int32, (cols, line), 1)

    def gradient(r, z):
        grad_out[0, r] = (img_pad[r + 2, TILE : TILE + cols] - img_pad[r, TILE : TILE + cols]) * 0.5
        grad_out[1, r] = (
            img_pad[r + 1, TILE + 1 : TILE + cols + 1] - img_pad[r + 1, TILE - 1 : TILE + cols - 1]
        ) * 0.5
        center = img_pad[r + 1, TILE : TILE + cols]
        after = jnp.where(lane == line - 1, 0.0, pltpu.roll(center, line - 1, 1))
        before = jnp.where(lane == 0, 0.0, pltpu.roll(center, 1, 1))
        grad_out[2, r] = (after - before) * 0.5
        return z

    lax.fori_loop(0, rows, gradient, 0)

    def finish(c, z):
        combine_out = combine(total - chunks + c, c)
        acc[c] = combine_out.reshape(tall, TILE, width)
        back_tx[c] = acc[c, pl.ds(other * rows, rows)]
        back_copy(c).start()
        adj_out[(slice(None),) + place(c, y)] = acc[c, pl.ds(y * rows, rows)]
        return z

    lax.fori_loop(0, chunks, finish, 0)

    def collect(c, z):
        back_copy(c).wait_recv()
        adj_out[(slice(None),) + place(c, other)] = back_rx[c]
        return z

    lax.fori_loop(0, chunks, collect, 0)

    dep_remote(y).wait_send()
    lax.fori_loop(0, chunks, lambda c, z: (cur_remote(c, y).wait_send(), back_copy(c).wait_send(), z)[2], 0)

    def drain(t, z):
        frac_remote(t, y).wait_send()

        @pl.when(has_upper)
        def _():
            up_copy(t).wait_send()

        @pl.when(has_lower)
        def _():
            dn_copy(t).wait_send()

        return z

    lax.fori_loop(0, total, drain, 0)
    for send, _, copy in halos:
        @pl.when(send)
        def _():
            copy.wait_send()


def shards(slabs, pencils, final_adjoint, departure, fraction, image):
    steps, rows, cols = departure.shape
    line = image.shape[2]
    half = line // 2
    width = WIDTH if half % WIDTH == 0 else half
    tiles = cols // TILE
    chunks = tiles * (half // width)
    total = steps * chunks
    tall = 2 * rows
    assert slabs % 2 == 0 and ABOVE <= tall and cols % (2 * TILE) == 0 and half % 128 == 0

    f32 = jnp.float32
    dma = pltpu.SemaphoreType.DMA
    vmem = pl.BlockSpec(memory_space=pltpu.VMEM)
    hbm = pl.BlockSpec(memory_space=pltpu.HBM)
    adjoint, gradient = pl.pallas_call(
        functools.partial(kernel, slabs, pencils),
        name="splat",
        out_shape=(
            jax.ShapeDtypeStruct((rows, cols, line), f32),
            jax.ShapeDtypeStruct((3, rows, cols, line), f32),
        ),
        in_specs=[hbm, hbm, hbm, hbm],
        out_specs=(vmem, vmem),
        scratch_shapes=[
            pltpu.VMEM((2, steps, rows, cols), jnp.int32),
            pltpu.VMEM((2, tiles, steps, 4 * rows * TILE), jnp.int32),
            pltpu.VMEM((rows, cols, line), jnp.bfloat16),
            pltpu.VMEM((2, chunks, rows, TILE, width), f32),
            pltpu.VMEM((chunks, 2, rows, TILE, width), f32),
            pltpu.VMEM((total, 2, rows, TILE, width), f32),
            pltpu.VMEM((chunks, tall, TILE, width), f32),
            pltpu.VMEM((total, ABOVE, TILE, width), f32),
            pltpu.VMEM((total, BELOW, TILE, width), f32),
            pltpu.VMEM((total, ABOVE, TILE, width), f32),
            pltpu.VMEM((total, BELOW, TILE, width), f32),
            pltpu.VMEM((chunks, rows, TILE, width), f32),
            pltpu.VMEM((chunks, rows, TILE, width), f32),
            pltpu.VMEM((rows + 2, cols + 2 * TILE, line), f32),
            dma((2,)),
            dma(()),
            dma(()),
            dma((2, chunks)),
            dma((total,)),
            dma((2, total)),
            dma((2, total)),
            dma((2, total)),
            dma((2, chunks)),
            dma(()),
            dma((2, 4)),
        ],
        compiler_params=pltpu.CompilerParams(
            collective_id=0, has_side_effects=True, vmem_limit_bytes=40 * 1024 * 1024
        ),
    )(*(pltpu.with_memory_space_constraint(a, pltpu.HBM) for a in (departure, final_adjoint, fraction, image)))
    return adjoint.astype(jnp.bfloat16), adjoint[None] * gradient


def solution(mesh):
    in_specs = (
        P("slab", "pencil", None),
        P(None, "slab", "pencil"),
        P(None, "slab", "pencil", None),
        P("slab", "pencil", None),
    )
    out_specs = (P("slab", "pencil", None), P(None, "slab", "pencil", None))
    body = functools.partial(shards, mesh.shape["slab"], mesh.shape["pencil"])
    return jax.shard_map(body, mesh=mesh, in_specs=in_specs, out_specs=out_specs, check_vma=False)
```

```python
import functools

import jax
import jax.numpy as jnp
from jax import lax
from jax.experimental import pallas as pl
from jax.experimental.pallas import tpu as pltpu
from jax.sharding import PartitionSpec as P

BELOW = 5
ABOVE = 6
TILE = 8
AHEAD = 4
WIDTH = 256
MESH = pl.DeviceIdType.MESH


def kernel(
    slabs,
    pencils,
    dep_ref,
    adj_ref,
    frac_ref,
    img_ref,
    adj_out,
    grad_out,
    dep_buf,
    land_buf,
    adj_buf,
    stage,
    cur,
    frac_buf,
    acc,
    tx_up,
    tx_dn,
    rx_lo,
    rx_hi,
    back_tx,
    back_rx,
    img_pad,
    relay_buf,
    dep_sem,
    own_dep_sem,
    adj_sem,
    cur_sem,
    fl_sem,
    fr_sem,
    up_sem,
    dn_sem,
    back_sem,
    img_sem,
    halo_sem,
):
    s = lax.axis_index("slab")
    p = lax.axis_index("pencil")
    y = lax.rem(s, 2)
    other = 1 - y
    partner = s + 1 - 2 * y
    pair = lax.div(s, 2)
    has_lower = s >= 2
    has_upper = s + 2 < slabs

    rows, cols, line = adj_out.shape
    half = line // 2
    width = stage.shape[-1]
    lanes_parts = half // width
    tiles = cols // TILE
    chunks = tiles * lanes_parts
    steps = frac_ref.shape[0]
    total = steps * chunks
    ahead = chunks + chunks * AHEAD // 8
    tall = 2 * rows
    span = BELOW + tall + ABOVE

    def remote(src, dst, sems, index, where):
        return pltpu.make_async_remote_copy(
            src_ref=src,
            dst_ref=dst,
            send_sem=sems.at[(0,) + index],
            recv_sem=sems.at[(1,) + index],
            device_id=where,
            device_id_type=MESH,
        )

    def place(c, side):
        first = pl.multiple_of(lax.div(c, lanes_parts) * TILE, TILE)
        lanes = pl.multiple_of(side * half + lax.rem(c, lanes_parts) * width, width)
        return pl.ds(first, TILE), pl.ds(lanes, width)

    def frac_block(t, side):
        step = steps - 1 - lax.div(t, chunks)
        return frac_ref.at[(step, slice(None)) + place(lax.rem(t, chunks), side)]

    def frac_local(t):
        return pltpu.make_async_copy(frac_block(t, y), frac_buf.at[t, y], fl_sem.at[t])

    def frac_remote(t, slot):
        return remote(frac_block(t, other), frac_buf.at[t, slot], fr_sem, (t,), {"slab": partner})

    def cur_remote(c, slot):
        return remote(stage.at[other, c], cur.at[c, slot], cur_sem, (c,), {"slab": partner})

    def dep_remote(slot):
        return remote(dep_ref, dep_buf.at[slot], dep_sem, (), {"slab": partner})

    def up_copy(t):
        return remote(tx_up.at[t], rx_lo.at[t], up_sem, (t,), {"slab": s + 2})

    def dn_copy(t):
        return remote(tx_dn.at[t], rx_hi.at[t], dn_sem, (t,), {"slab": s - 2})

    def back_copy(c):
        return remote(back_tx.at[c], back_rx.at[c], back_sem, (c,), {"slab": partner})

    center_cols = pl.ds(TILE, cols)
    image_copy = pltpu.make_async_copy(
        img_ref, img_pad.at[pl.ds(1, rows), center_cols], img_sem
    )
    relay_to = s + 4 * y - 2
    relay_from = s + 2 - 4 * y
    outer = s + 2 * y - 1
    sends_relay = jnp.logical_and(relay_to >= 0, relay_to < slabs)
    gets_relay = jnp.logical_and(relay_from >= 0, relay_from < slabs)
    gets_outer = jnp.logical_and(outer >= 0, outer < slabs)
    relay_copy = remote(
        img_ref.at[pl.ds(y * (rows - 1), 1)], relay_buf, halo_sem, (0,), {"slab": relay_to}
    )
    outer_copy = remote(
        relay_buf, img_pad.at[pl.ds(other * (rows + 1), 1), center_cols], halo_sem, (1,), {"slab": partner}
    )
    inner_copy = remote(
        img_ref.at[pl.ds(other * (rows - 1), 1)], img_pad.at[pl.ds(y * (rows + 1), 1), center_cols],
        halo_sem, (4,), {"slab": partner}
    )
    halos = (
        (p + 1 < pencils, p >= 1, remote(
            img_ref.at[:, pl.ds(cols - TILE, TILE)], img_pad.at[pl.ds(1, rows), pl.ds(0, TILE)],
            halo_sem, (2,), {"pencil": p + 1})),
        (p >= 1, p + 1 < pencils, remote(
            img_ref.at[:, pl.ds(0, TILE)], img_pad.at[pl.ds(1, rows), pl.ds(cols + TILE, TILE)],
            halo_sem, (3,), {"pencil": p - 1})),
    )

    barrier = pltpu.get_barrier_semaphore()
    for there, where in (
        (slabs > 1, {"slab": partner}),
        (has_lower, {"slab": s - 2}),
        (has_upper, {"slab": s + 2}),
        (p >= 1, {"pencil": p - 1}),
        (p + 1 < pencils, {"pencil": p + 1}),
    ):
        @pl.when(there)
        def _():
            pl.semaphore_signal(barrier, inc=1, device_id=where, device_id_type=MESH)

    adj_copy = pltpu.make_async_copy(adj_ref, adj_buf, adj_sem)
    dep_copy = pltpu.make_async_copy(dep_ref, dep_buf.at[y], own_dep_sem)
    dep_copy.start()
    adj_copy.start()
    lax.fori_loop(0, total, lambda t, z: (frac_local(t).start(), z)[1], 0)
    image_copy.start()
    adj_copy.wait()
    for q in range(cols // (2 * TILE)):
        for h in range(2):
            for k in range(lanes_parts):
                first = half * h + width * k
                wide = adj_buf[:, 2 * TILE * q : 2 * TILE * (q + 1), first : first + width]
                wide = wide.astype(jnp.float32)
                stage[h, 2 * q * lanes_parts + k] = wide[:, :TILE]
                stage[h, (2 * q + 1) * lanes_parts + k] = wide[:, TILE:]

    peers = sum(
        jnp.where(there, 1, 0)
        for there in (slabs > 1, has_lower, has_upper, p >= 1, p + 1 < pencils)
    )
    pl.semaphore_wait(barrier, peers)

    dep_remote(y).start()

    @pl.when(sends_relay)
    def _():
        relay_copy.start()

    def start_first(c, z):
        frac_remote(c, y).start()
        cur_remote(c, y).start()
        return z

    lax.fori_loop(0, chunks, start_first, 0)
    for send, _, copy in halos:
        @pl.when(send)
        def _():
            copy.start()
    lax.fori_loop(chunks, ahead, lambda t, z: (frac_remote(t, y).start(), z)[1], 0)

    for c in range(chunks):
        cur[c, y] = stage[y, c]

    lane = lax.broadcasted_iota(jnp.int32, (steps, 4 * rows * TILE), 1)
    lane_row = lax.rem(lax.div(lane, TILE), rows)
    fixed = lane_row + lax.div(lane, rows * TILE) - 1 + BELOW
    fixed = fixed * TILE + lax.rem(lane, TILE)
    pick_lane = lax.broadcasted_iota(jnp.int32, (cols, 4 * rows * TILE), 1)
    pick_col = lax.broadcasted_iota(jnp.int32, (cols, 4 * rows * TILE), 0)
    keep_lane = lax.broadcasted_iota(jnp.int32, (steps * rows, 4 * rows * TILE), 1)
    keep_row = lax.broadcasted_iota(jnp.int32, (steps * rows, 4 * rows * TILE), 0)
    keep = lax.rem(keep_row, rows) == lax.rem(lax.div(keep_lane, TILE), rows)
    group_step = lax.broadcasted_iota(jnp.int32, (steps, steps * rows), 0)
    group_row = lax.broadcasted_iota(jnp.int32, (steps, steps * rows), 1)
    group = jnp.where(group_step == lax.div(group_row, rows), 1.0, 0.0).astype(jnp.bfloat16)
    row_of = lax.broadcasted_iota(jnp.int32, (rows, cols), 0)

    def landing(h):
        first_row = pair * tall + h * rows
        moved = jnp.concatenate([dep_buf[h, k] - row_of - first_row for k in range(steps)], axis=0)
        moved = moved.astype(jnp.float32).astype(jnp.bfloat16)
        for tile in range(tiles):
            pick = pick_col == tile * TILE + lax.rem(pick_lane, TILE)
            pick = jnp.where(pick, 1.0, 0.0).astype(jnp.bfloat16)
            spread = jnp.dot(moved, pick, preferred_element_type=jnp.float32)
            spread = jnp.where(keep, spread, 0.0).astype(jnp.bfloat16)
            by_step = jnp.dot(group, spread, preferred_element_type=jnp.float32)
            land_buf[h, tile] = fixed + h * rows * TILE + by_step.astype(jnp.int32) * TILE

    dep_copy.wait()
    landing(y)
    dep_remote(other).wait_recv()
    landing(other)

    def splat(t, c, values):
        frac_local(t).wait()
        frac_remote(t, other).wait_recv()
        parts = []
        hots = []
        target = lax.broadcasted_iota(jnp.int32, (span * TILE, 4 * rows * TILE), 0)
        tile = lax.div(c, lanes_parts)
        step = steps - 1 - lax.div(t, chunks)
        for h in range(2):
            f = frac_buf[t, h].reshape(rows * TILE, width)
            v = values[h].reshape(rows * TILE, width)
            rest = 1.0 - f
            square = f * f
            cube = square * f
            sixth = v * (1.0 / 6.0)
            parts.append(rest * rest * rest * sixth)
            parts.append((3.0 * cube - 6.0 * square + 4.0) * sixth)
            parts.append((-3.0 * cube + 3.0 * square + 3.0 * f + 1.0) * sixth)
            parts.append(cube * sixth)
            land = land_buf[h, tile, pl.ds(step, 1), :]
            hots.append(jnp.where(target == land, 1.0, 0.0).astype(jnp.bfloat16))
        hot = jnp.concatenate(hots, axis=1)
        high = [part.astype(jnp.bfloat16) for part in parts]
        low = [(a - b.astype(jnp.float32)).astype(jnp.bfloat16) for a, b in zip(parts, high)]
        out = jnp.dot(hot, jnp.concatenate(high, axis=0), preferred_element_type=jnp.float32)
        out = out + jnp.dot(hot, jnp.concatenate(low, axis=0), preferred_element_type=jnp.float32)
        out = out.reshape(span, TILE, width)
        tx_dn[t] = out[:BELOW]
        tx_up[t] = out[BELOW + tall :]

        @pl.when(has_upper)
        def _():
            up_copy(t).start()

        @pl.when(has_lower)
        def _():
            dn_copy(t).start()

        acc[c] = out[BELOW : BELOW + tall]

    def combine(t, c):
        @pl.when(has_lower)
        def _():
            up_copy(t).wait_recv()
            acc[c, :ABOVE] += rx_lo[t]

        @pl.when(has_upper)
        def _():
            dn_copy(t).wait_recv()
            acc[c, tall - BELOW :] += rx_hi[t]

        whole = acc[c].astype(jnp.bfloat16).astype(jnp.float32)
        return whole.reshape(2, rows, TILE, width)

    def first_step(c, z):
        cur_remote(c, other).wait_recv()
        splat(c, c, cur[c])
        frac_remote(c + ahead, y).start()
        return z

    lax.fori_loop(0, chunks, first_step, 0)

    def later_step(t, z):
        c = lax.rem(t, chunks)
        splat(t, c, combine(t - chunks, c))
        return z

    def paced_step(t, z):
        frac_remote(t + ahead, y).start()
        return later_step(t, z)

    lax.fori_loop(chunks, total - ahead, paced_step, 0)
    @pl.when(gets_relay)
    def _():
        relay_copy.wait_recv()
        outer_copy.start()

    inner_copy.start()

    lax.fori_loop(total - ahead, total, later_step, 0)

    image_copy.wait()
    inner_copy.wait_recv()

    @pl.when(gets_outer)
    def _():
        outer_copy.wait_recv()

    @pl.when(jnp.logical_not(gets_outer))
    def _():
        img_pad[y * (rows + 1), TILE : TILE + cols] = jnp.zeros((cols, line), jnp.float32)

    for index, (_, receive, copy) in enumerate(halos):
        @pl.when(receive)
        def _():
            copy.wait_recv()

        @pl.when(jnp.logical_not(receive))
        def _():
            edge = 0 if index == 0 else cols + TILE
            img_pad[1 : rows + 1, edge : edge + TILE] = jnp.zeros((rows, TILE, line), jnp.float32)

    lane = lax.broadcasted_iota(jnp.int32, (cols, line), 1)

    def gradient(r, z):
        grad_out[0, r] = (img_pad[r + 2, TILE : TILE + cols] - img_pad[r, TILE : TILE + cols]) * 0.5
        grad_out[1, r] = (
            img_pad[r + 1, TILE + 1 : TILE + cols + 1] - img_pad[r + 1, TILE - 1 : TILE + cols - 1]
        ) * 0.5
        center = img_pad[r + 1, TILE : TILE + cols]
        after = jnp.where(lane == line - 1, 0.0, pltpu.roll(center, line - 1, 1))
        before = jnp.where(lane == 0, 0.0, pltpu.roll(center, 1, 1))
        grad_out[2, r] = (after - before) * 0.5
        return z

    lax.fori_loop(0, rows, gradient, 0)

    def finish(c, z):
        combine_out = combine(total - chunks + c, c)
        acc[c] = combine_out.reshape(tall, TILE, width)
        back_tx[c] = acc[c, pl.ds(other * rows, rows)]
        back_copy(c).start()
        adj_out[(slice(None),) + place(c, y)] = acc[c, pl.ds(y * rows, rows)]
        return z

    lax.fori_loop(0, chunks, finish, 0)

    def collect(c, z):
        back_copy(c).wait_recv()
        adj_out[(slice(None),) + place(c, other)] = back_rx[c]
        return z

    lax.fori_loop(0, chunks, collect, 0)

    dep_remote(y).wait_send()
    lax.fori_loop(0, chunks, lambda c, z: (cur_remote(c, y).wait_send(), back_copy(c).wait_send(), z)[2], 0)

    def drain(t, z):
        frac_remote(t, y).wait_send()

        @pl.when(has_upper)
        def _():
            up_copy(t).wait_send()

        @pl.when(has_lower)
        def _():
            dn_copy(t).wait_send()

        return z

    lax.fori_loop(0, total, drain, 0)
    inner_copy.wait_send()

    @pl.when(sends_relay)
    def _():
        relay_copy.wait_send()

    @pl.when(gets_relay)
    def _():
        outer_copy.wait_send()

    for send, _, copy in halos:
        @pl.when(send)
        def _():
            copy.wait_send()


def shards(slabs, pencils, final_adjoint, departure, fraction, image):
    steps, rows, cols = departure.shape
    line = image.shape[2]
    half = line // 2
    width = WIDTH if half % WIDTH == 0 else half
    tiles = cols // TILE
    chunks = tiles * (half // width)
    total = steps * chunks
    tall = 2 * rows
    assert slabs % 2 == 0 and ABOVE <= tall and cols % (2 * TILE) == 0 and half % 128 == 0

    f32 = jnp.float32
    dma = pltpu.SemaphoreType.DMA
    vmem = pl.BlockSpec(memory_space=pltpu.VMEM)
    hbm = pl.BlockSpec(memory_space=pltpu.HBM)
    adjoint, gradient = pl.pallas_call(
        functools.partial(kernel, slabs, pencils),
        name="splat",
        out_shape=(
            jax.ShapeDtypeStruct((rows, cols, line), f32),
            jax.ShapeDtypeStruct((3, rows, cols, line), f32),
        ),
        in_specs=[hbm, hbm, hbm, hbm],
        out_specs=(vmem, vmem),
        scratch_shapes=[
            pltpu.VMEM((2, steps, rows, cols), jnp.int32),
            pltpu.VMEM((2, tiles, steps, 4 * rows * TILE), jnp.int32),
            pltpu.VMEM((rows, cols, line), jnp.bfloat16),
            pltpu.VMEM((2, chunks, rows, TILE, width), f32),
            pltpu.VMEM((chunks, 2, rows, TILE, width), f32),
            pltpu.VMEM((total, 2, rows, TILE, width), f32),
            pltpu.VMEM((chunks, tall, TILE, width), f32),
            pltpu.VMEM((total, ABOVE, TILE, width), f32),
            pltpu.VMEM((total, BELOW, TILE, width), f32),
            pltpu.VMEM((total, ABOVE, TILE, width), f32),
            pltpu.VMEM((total, BELOW, TILE, width), f32),
            pltpu.VMEM((chunks, rows, TILE, width), f32),
            pltpu.VMEM((chunks, rows, TILE, width), f32),
            pltpu.VMEM((rows + 2, cols + 2 * TILE, line), f32),
            pltpu.VMEM((1, cols, line), f32),
            dma((2,)),
            dma(()),
            dma(()),
            dma((2, chunks)),
            dma((total,)),
            dma((2, total)),
            dma((2, total)),
            dma((2, total)),
            dma((2, chunks)),
            dma(()),
            dma((2, 5)),
        ],
        compiler_params=pltpu.CompilerParams(
            collective_id=0, has_side_effects=True, vmem_limit_bytes=40 * 1024 * 1024
        ),
    )(*(pltpu.with_memory_space_constraint(a, pltpu.HBM) for a in (departure, final_adjoint, fraction, image)))
    return adjoint.astype(jnp.bfloat16), adjoint[None] * gradient


def solution(mesh):
    in_specs = (
        P("slab", "pencil", None),
        P(None, "slab", "pencil"),
        P(None, "slab", "pencil", None),
        P("slab", "pencil", None),
    )
    out_specs = (P("slab", "pencil", None), P(None, "slab", "pencil", None))
    body = functools.partial(shards, mesh.shape["slab"], mesh.shape["pencil"])
    return jax.shard_map(body, mesh=mesh, in_specs=in_specs, out_specs=out_specs, check_vma=False)
```

```python
import functools

import jax
import jax.numpy as jnp
from jax import lax
from jax.experimental import pallas as pl
from jax.experimental.pallas import tpu as pltpu
from jax.sharding import PartitionSpec as P

BELOW = 5
ABOVE = 6
TILE = 8
AHEAD = 4
WIDTH = 512
MESH = pl.DeviceIdType.MESH


def kernel(
    slabs,
    pencils,
    dep_ref,
    adj_ref,
    frac_ref,
    img_ref,
    adj_out,
    grad_out,
    dep_buf,
    land_buf,
    adj_buf,
    stage,
    cur,
    frac_buf,
    acc,
    tx_up,
    tx_dn,
    rx_lo,
    rx_hi,
    back_tx,
    back_rx,
    img_pad,
    relay_buf,
    dep_sem,
    own_dep_sem,
    adj_sem,
    cur_sem,
    fl_sem,
    fr_sem,
    up_sem,
    dn_sem,
    back_sem,
    img_sem,
    halo_sem,
):
    s = lax.axis_index("slab")
    p = lax.axis_index("pencil")
    y = lax.rem(s, 2)
    other = 1 - y
    partner = s + 1 - 2 * y
    pair = lax.div(s, 2)
    has_lower = s >= 2
    has_upper = s + 2 < slabs

    rows, cols, line = adj_out.shape
    half = line // 2
    width = stage.shape[-1]
    lanes_parts = half // width
    tiles = cols // TILE
    chunks = tiles * lanes_parts
    steps = frac_ref.shape[0]
    total = steps * chunks
    ahead = chunks + chunks * AHEAD // 8
    tall = 2 * rows
    span = BELOW + tall + ABOVE

    def remote(src, dst, sems, index, where):
        return pltpu.make_async_remote_copy(
            src_ref=src,
            dst_ref=dst,
            send_sem=sems.at[(0,) + index],
            recv_sem=sems.at[(1,) + index],
            device_id=where,
            device_id_type=MESH,
        )

    def place(c, side):
        first = pl.multiple_of(lax.div(c, lanes_parts) * TILE, TILE)
        lanes = pl.multiple_of(side * half + lax.rem(c, lanes_parts) * width, width)
        return pl.ds(first, TILE), pl.ds(lanes, width)

    def frac_block(t, side):
        step = steps - 1 - lax.div(t, chunks)
        return frac_ref.at[(step, slice(None)) + place(lax.rem(t, chunks), side)]

    def frac_local(t):
        return pltpu.make_async_copy(frac_block(t, y), frac_buf.at[t, y], fl_sem.at[t])

    def frac_remote(t, slot):
        return remote(frac_block(t, other), frac_buf.at[t, slot], fr_sem, (t,), {"slab": partner})

    def cur_remote(c, slot):
        return remote(stage.at[other, c], cur.at[c, slot], cur_sem, (c,), {"slab": partner})

    def dep_remote(slot):
        return remote(dep_ref, dep_buf.at[slot], dep_sem, (), {"slab": partner})

    def up_copy(t):
        return remote(tx_up.at[t], rx_lo.at[t], up_sem, (t,), {"slab": s + 2})

    def dn_copy(t):
        return remote(tx_dn.at[t], rx_hi.at[t], dn_sem, (t,), {"slab": s - 2})

    def back_copy(c):
        return remote(back_tx.at[c], back_rx.at[c], back_sem, (c,), {"slab": partner})

    center_cols = pl.ds(TILE, cols)
    image_copy = pltpu.make_async_copy(
        img_ref, img_pad.at[pl.ds(1, rows), center_cols], img_sem
    )
    relay_to = s + 4 * y - 2
    relay_from = s + 2 - 4 * y
    outer = s + 2 * y - 1
    sends_relay = jnp.logical_and(relay_to >= 0, relay_to < slabs)
    gets_relay = jnp.logical_and(relay_from >= 0, relay_from < slabs)
    gets_outer = jnp.logical_and(outer >= 0, outer < slabs)
    relay_copy = remote(
        img_ref.at[pl.ds(y * (rows - 1), 1)], relay_buf, halo_sem, (0,), {"slab": relay_to}
    )
    outer_copy = remote(
        relay_buf, img_pad.at[pl.ds(other * (rows + 1), 1), center_cols], halo_sem, (1,), {"slab": partner}
    )
    inner_copy = remote(
        img_ref.at[pl.ds(other * (rows - 1), 1)], img_pad.at[pl.ds(y * (rows + 1), 1), center_cols],
        halo_sem, (4,), {"slab": partner}
    )
    halos = (
        (p + 1 < pencils, p >= 1, remote(
            img_ref.at[:, pl.ds(cols - TILE, TILE)], img_pad.at[pl.ds(1, rows), pl.ds(0, TILE)],
            halo_sem, (2,), {"pencil": p + 1})),
        (p >= 1, p + 1 < pencils, remote(
            img_ref.at[:, pl.ds(0, TILE)], img_pad.at[pl.ds(1, rows), pl.ds(cols + TILE, TILE)],
            halo_sem, (3,), {"pencil": p - 1})),
    )

    barrier = pltpu.get_barrier_semaphore()
    for there, where in (
        (slabs > 1, {"slab": partner}),
        (has_lower, {"slab": s - 2}),
        (has_upper, {"slab": s + 2}),
        (p >= 1, {"pencil": p - 1}),
        (p + 1 < pencils, {"pencil": p + 1}),
    ):
        @pl.when(there)
        def _():
            pl.semaphore_signal(barrier, inc=1, device_id=where, device_id_type=MESH)

    adj_copy = pltpu.make_async_copy(adj_ref, adj_buf, adj_sem)
    dep_copy = pltpu.make_async_copy(dep_ref, dep_buf.at[y], own_dep_sem)
    dep_copy.start()
    adj_copy.start()
    lax.fori_loop(0, total, lambda t, z: (frac_local(t).start(), z)[1], 0)
    image_copy.start()
    adj_copy.wait()
    for q in range(cols // (2 * TILE)):
        for h in range(2):
            for k in range(lanes_parts):
                first = half * h + width * k
                wide = adj_buf[:, 2 * TILE * q : 2 * TILE * (q + 1), first : first + width]
                wide = wide.astype(jnp.float32)
                stage[h, 2 * q * lanes_parts + k] = wide[:, :TILE]
                stage[h, (2 * q + 1) * lanes_parts + k] = wide[:, TILE:]

    peers = sum(
        jnp.where(there, 1, 0)
        for there in (slabs > 1, has_lower, has_upper, p >= 1, p + 1 < pencils)
    )
    pl.semaphore_wait(barrier, peers)

    dep_remote(y).start()

    @pl.when(sends_relay)
    def _():
        relay_copy.start()

    def start_first(c, z):
        frac_remote(c, y).start()
        cur_remote(c, y).start()
        return z

    lax.fori_loop(0, chunks, start_first, 0)
    for send, _, copy in halos:
        @pl.when(send)
        def _():
            copy.start()
    lax.fori_loop(chunks, ahead, lambda t, z: (frac_remote(t, y).start(), z)[1], 0)

    for c in range(chunks):
        cur[c, y] = stage[y, c]

    lane = lax.broadcasted_iota(jnp.int32, (steps, 4 * rows * TILE), 1)
    lane_row = lax.rem(lax.div(lane, TILE), rows)
    fixed = lane_row + lax.div(lane, rows * TILE) - 1 + BELOW
    fixed = fixed * TILE + lax.rem(lane, TILE)
    pick_lane = lax.broadcasted_iota(jnp.int32, (cols, 4 * rows * TILE), 1)
    pick_col = lax.broadcasted_iota(jnp.int32, (cols, 4 * rows * TILE), 0)
    keep_lane = lax.broadcasted_iota(jnp.int32, (steps * rows, 4 * rows * TILE), 1)
    keep_row = lax.broadcasted_iota(jnp.int32, (steps * rows, 4 * rows * TILE), 0)
    keep = lax.rem(keep_row, rows) == lax.rem(lax.div(keep_lane, TILE), rows)
    group_step = lax.broadcasted_iota(jnp.int32, (steps, steps * rows), 0)
    group_row = lax.broadcasted_iota(jnp.int32, (steps, steps * rows), 1)
    group = jnp.where(group_step == lax.div(group_row, rows), 1.0, 0.0).astype(jnp.bfloat16)
    row_of = lax.broadcasted_iota(jnp.int32, (rows, cols), 0)

    def landing(h):
        first_row = pair * tall + h * rows
        moved = jnp.concatenate([dep_buf[h, k] - row_of - first_row for k in range(steps)], axis=0)
        moved = moved.astype(jnp.float32).astype(jnp.bfloat16)
        for tile in range(tiles):
            pick = pick_col == tile * TILE + lax.rem(pick_lane, TILE)
            pick = jnp.where(pick, 1.0, 0.0).astype(jnp.bfloat16)
            spread = jnp.dot(moved, pick, preferred_element_type=jnp.float32)
            spread = jnp.where(keep, spread, 0.0).astype(jnp.bfloat16)
            by_step = jnp.dot(group, spread, preferred_element_type=jnp.float32)
            land_buf[h, tile] = fixed + h * rows * TILE + by_step.astype(jnp.int32) * TILE

    dep_copy.wait()
    landing(y)
    dep_remote(other).wait_recv()
    landing(other)

    def splat(t, c, values):
        frac_local(t).wait()
        frac_remote(t, other).wait_recv()
        parts = []
        hots = []
        target = lax.broadcasted_iota(jnp.int32, (span * TILE, 4 * rows * TILE), 0)
        tile = lax.div(c, lanes_parts)
        step = steps - 1 - lax.div(t, chunks)
        for h in range(2):
            f = frac_buf[t, h].reshape(rows * TILE, width)
            v = values[h].reshape(rows * TILE, width)
            rest = 1.0 - f
            square = f * f
            cube = square * f
            sixth = v * (1.0 / 6.0)
            parts.append(rest * rest * rest * sixth)
            parts.append((3.0 * cube - 6.0 * square + 4.0) * sixth)
            parts.append((-3.0 * cube + 3.0 * square + 3.0 * f + 1.0) * sixth)
            parts.append(cube * sixth)
            land = land_buf[h, tile, pl.ds(step, 1), :]
            hots.append(jnp.where(target == land, 1.0, 0.0).astype(jnp.bfloat16))
        hot = jnp.concatenate(hots, axis=1)
        high = [part.astype(jnp.bfloat16) for part in parts]
        low = [(a - b.astype(jnp.float32)).astype(jnp.bfloat16) for a, b in zip(parts, high)]
        out = jnp.dot(hot, jnp.concatenate(high, axis=0), preferred_element_type=jnp.float32)
        out = out + jnp.dot(hot, jnp.concatenate(low, axis=0), preferred_element_type=jnp.float32)
        out = out.reshape(span, TILE, width)
        tx_dn[t] = out[:BELOW]
        tx_up[t] = out[BELOW + tall :]

        @pl.when(has_upper)
        def _():
            up_copy(t).start()

        @pl.when(has_lower)
        def _():
            dn_copy(t).start()

        acc[c] = out[BELOW : BELOW + tall]

    def combine(t, c):
        @pl.when(has_lower)
        def _():
            up_copy(t).wait_recv()
            acc[c, :ABOVE] += rx_lo[t]

        @pl.when(has_upper)
        def _():
            dn_copy(t).wait_recv()
            acc[c, tall - BELOW :] += rx_hi[t]

        whole = acc[c].astype(jnp.bfloat16).astype(jnp.float32)
        return whole.reshape(2, rows, TILE, width)

    def first_step(c, z):
        cur_remote(c, other).wait_recv()
        splat(c, c, cur[c])
        frac_remote(c + ahead, y).start()
        return z

    lax.fori_loop(0, chunks, first_step, 0)

    def later_step(t, z):
        c = lax.rem(t, chunks)
        splat(t, c, combine(t - chunks, c))
        return z

    def paced_step(t, z):
        frac_remote(t + ahead, y).start()
        return later_step(t, z)

    lax.fori_loop(chunks, total - ahead, paced_step, 0)
    @pl.when(gets_relay)
    def _():
        relay_copy.wait_recv()
        outer_copy.start()

    inner_copy.start()

    lax.fori_loop(total - ahead, total, later_step, 0)

    image_copy.wait()
    inner_copy.wait_recv()

    @pl.when(gets_outer)
    def _():
        outer_copy.wait_recv()

    @pl.when(jnp.logical_not(gets_outer))
    def _():
        img_pad[y * (rows + 1), TILE : TILE + cols] = jnp.zeros((cols, line), jnp.float32)

    for index, (_, receive, copy) in enumerate(halos):
        @pl.when(receive)
        def _():
            copy.wait_recv()

        @pl.when(jnp.logical_not(receive))
        def _():
            edge = 0 if index == 0 else cols + TILE
            img_pad[1 : rows + 1, edge : edge + TILE] = jnp.zeros((rows, TILE, line), jnp.float32)

    lane = lax.broadcasted_iota(jnp.int32, (cols, line), 1)

    def gradient(r, z):
        grad_out[0, r] = (img_pad[r + 2, TILE : TILE + cols] - img_pad[r, TILE : TILE + cols]) * 0.5
        grad_out[1, r] = (
            img_pad[r + 1, TILE + 1 : TILE + cols + 1] - img_pad[r + 1, TILE - 1 : TILE + cols - 1]
        ) * 0.5
        center = img_pad[r + 1, TILE : TILE + cols]
        after = jnp.where(lane == line - 1, 0.0, pltpu.roll(center, line - 1, 1))
        before = jnp.where(lane == 0, 0.0, pltpu.roll(center, 1, 1))
        grad_out[2, r] = (after - before) * 0.5
        return z

    lax.fori_loop(0, rows, gradient, 0)

    def finish(c, z):
        combine_out = combine(total - chunks + c, c)
        acc[c] = combine_out.reshape(tall, TILE, width)
        back_tx[c] = acc[c, pl.ds(other * rows, rows)]
        back_copy(c).start()
        mine = acc[c, pl.ds(y * rows, rows)]
        adj_out[(slice(None),) + place(c, y)] = mine
        grad_out[(slice(None), slice(None)) + place(c, y)] *= mine[None]
        return z

    lax.fori_loop(0, chunks, finish, 0)

    def collect(c, z):
        back_copy(c).wait_recv()
        adj_out[(slice(None),) + place(c, other)] = back_rx[c]
        grad_out[(slice(None), slice(None)) + place(c, other)] *= back_rx[c][None]
        return z

    lax.fori_loop(0, chunks, collect, 0)

    dep_remote(y).wait_send()
    lax.fori_loop(0, chunks, lambda c, z: (cur_remote(c, y).wait_send(), back_copy(c).wait_send(), z)[2], 0)

    def drain(t, z):
        frac_remote(t, y).wait_send()

        @pl.when(has_upper)
        def _():
            up_copy(t).wait_send()

        @pl.when(has_lower)
        def _():
            dn_copy(t).wait_send()

        return z

    lax.fori_loop(0, total, drain, 0)
    inner_copy.wait_send()

    @pl.when(sends_relay)
    def _():
        relay_copy.wait_send()

    @pl.when(gets_relay)
    def _():
        outer_copy.wait_send()

    for send, _, copy in halos:
        @pl.when(send)
        def _():
            copy.wait_send()


def shards(slabs, pencils, final_adjoint, departure, fraction, image):
    steps, rows, cols = departure.shape
    line = image.shape[2]
    half = line // 2
    width = WIDTH if half % WIDTH == 0 else half
    tiles = cols // TILE
    chunks = tiles * (half // width)
    total = steps * chunks
    tall = 2 * rows
    assert slabs % 2 == 0 and ABOVE <= tall and cols % (2 * TILE) == 0 and half % 128 == 0

    f32 = jnp.float32
    dma = pltpu.SemaphoreType.DMA
    vmem = pl.BlockSpec(memory_space=pltpu.VMEM)
    hbm = pl.BlockSpec(memory_space=pltpu.HBM)
    adjoint, gradient = pl.pallas_call(
        functools.partial(kernel, slabs, pencils),
        name="splat",
        out_shape=(
            jax.ShapeDtypeStruct((rows, cols, line), f32),
            jax.ShapeDtypeStruct((3, rows, cols, line), f32),
        ),
        in_specs=[hbm, hbm, hbm, hbm],
        out_specs=(vmem, vmem),
        scratch_shapes=[
            pltpu.VMEM((2, steps, rows, cols), jnp.int32),
            pltpu.VMEM((2, tiles, steps, 4 * rows * TILE), jnp.int32),
            pltpu.VMEM((rows, cols, line), jnp.bfloat16),
            pltpu.VMEM((2, chunks, rows, TILE, width), f32),
            pltpu.VMEM((chunks, 2, rows, TILE, width), f32),
            pltpu.VMEM((total, 2, rows, TILE, width), f32),
            pltpu.VMEM((chunks, tall, TILE, width), f32),
            pltpu.VMEM((total, ABOVE, TILE, width), f32),
            pltpu.VMEM((total, BELOW, TILE, width), f32),
            pltpu.VMEM((total, ABOVE, TILE, width), f32),
            pltpu.VMEM((total, BELOW, TILE, width), f32),
            pltpu.VMEM((chunks, rows, TILE, width), f32),
            pltpu.VMEM((chunks, rows, TILE, width), f32),
            pltpu.VMEM((rows + 2, cols + 2 * TILE, line), f32),
            pltpu.VMEM((1, cols, line), f32),
            dma((2,)),
            dma(()),
            dma(()),
            dma((2, chunks)),
            dma((total,)),
            dma((2, total)),
            dma((2, total)),
            dma((2, total)),
            dma((2, chunks)),
            dma(()),
            dma((2, 5)),
        ],
        compiler_params=pltpu.CompilerParams(
            collective_id=0, has_side_effects=True, vmem_limit_bytes=40 * 1024 * 1024
        ),
    )(*(pltpu.with_memory_space_constraint(a, pltpu.HBM) for a in (departure, final_adjoint, fraction, image)))
    return adjoint.astype(jnp.bfloat16), gradient


def solution(mesh):
    in_specs = (
        P("slab", "pencil", None),
        P(None, "slab", "pencil"),
        P(None, "slab", "pencil", None),
        P("slab", "pencil", None),
    )
    out_specs = (P("slab", "pencil", None), P(None, "slab", "pencil", None))
    body = functools.partial(shards, mesh.shape["slab"], mesh.shape["pencil"])
    return jax.shard_map(body, mesh=mesh, in_specs=in_specs, out_specs=out_specs, check_vma=False)
```
